32 devices in a mesh: lat: 4 (over z), lon: 8 (over y, x, core).
Axes of the slice: x: 2, y: 2, z: 4, core: 2. Of those that a mesh axis runs over, the one named last changes fastest.
Arguments:
- control: float32 [16, 137, 32, 1024], P('lon', None, 'lat'), may hold values from -6 to 6
- ensemble: bfloat16 [16, 137, 32, 1024], P(None, None, 'lat', 'lon'), may hold values from -2.5 to 2.5
- vertical_root: bfloat16 [137, 137], replicated, may hold values from -0.5 to 0.5
- sector_band: bfloat16 [3, 128, 1024], P(None, None, 'lon'), may hold values from -0.3125 to 0.3125
- latitude_taps: float32 [9, 1024], P(None, 'lon'), may hold values from -2 to 2
- innovation: float32 [137, 32, 1024], P(None, 'lat', 'lon'), may hold values from -6 to 6
- inverse_error: float32 [137, 32, 1024], P(None, 'lat', 'lon'), may hold values from 0.5 to 2
Outputs:
- gradient: float32 [16, 137, 32, 1024], P('lon', None, 'lat')
- departure: float32 [137, 32, 1024], P(None, 'lat', 'lon')
The draws below stay inside these ranges and needn't reach their ends.
All inputs are finite; a program needn't handle non-finite values.
Results may differ from the reference program's by a relative error of at most 0.007.
Values may be sent and summed in bfloat16 or wider, within the bound.
A program may use at most 128 MiB of HBM per device.

```python
import math
import jax
import jax.numpy as jnp
from jax import lax

MEMBERS = 16
LEVELS = 137
CX = 128
SPAN = 9
NY = 32
NX = 1024


def block_scale(rng, dims, shards, least, high):
    def one(position, blocks):
        draws = jax.random.uniform(jax.random.fold_in(jax.random.fold_in(rng, 6), position), (blocks,), jnp.float32, least / len(shards), high / len(shards))
        return jnp.repeat(jnp.exp(draws), dims[position] // blocks).reshape((-1,) + (1,) * (len(dims) - position - 1))

    gain = one(*shards[0])
    for cut in shards[1:]:
        gain = gain * one(*cut)
    return gain


def gaussian(rng, shape, scale, bound, shards=(), dtype=jnp.bfloat16):
    drawn = jax.random.normal(rng, shape, jnp.float32) * scale
    if len(shards) > 0:
        drawn = block_scale(rng, shape, shards, -0.22, 0.18) * drawn
    return jnp.clip(drawn, min=-bound, max=bound).astype(dtype)


def setup_inputs(seed: int = 0) -> dict:
    arg_keys = jax.random.split(jax.random.key(seed), 8)
    return {
        "control": gaussian(arg_keys[0], (MEMBERS, LEVELS, NY, NX), 1.0, 6.0, ((0, 8), (2, 4)), jnp.float32),
        "ensemble": gaussian(arg_keys[1], (MEMBERS, LEVELS, NY, NX), 0.35, 2.5, ((2, 4), (3, 8))),
        "vertical_root": gaussian(arg_keys[2], (LEVELS, LEVELS), LEVELS ** -0.5, 0.5),
        "sector_band": gaussian(arg_keys[3], (3, CX, NX), (3 * CX) ** -0.5, 0.3125, ((2, 8),)),
        "latitude_taps": gaussian(arg_keys[4], (SPAN, NX), SPAN ** -0.5, 2.0, ((1, 8),), jnp.float32),
        "innovation": gaussian(arg_keys[5], (LEVELS, NY, NX), 1.0, 6.0, ((1, 4), (2, 8)), jnp.float32),
        "inverse_error": jnp.clip(jnp.exp(math.log(2.0) - 1.3862944 * jax.random.uniform(arg_keys[6], (LEVELS, NY, NX), jnp.float32) ** block_scale(arg_keys[6], (LEVELS, NY, NX), ((1, 4), (2, 8)), -0.2, 0.2)), 0.5, 2.0),
    }


def blocked_band(sector_band):
    taps, width, total = sector_band.shape
    count = total // width
    return sector_band.reshape(taps, width, count, width).transpose(2, 0, 1, 3).reshape(count, taps * width, width)


def reference(control, ensemble, vertical_root, sector_band, latitude_taps, innovation, inverse_error):
    levels, height, total = innovation.shape
    width = sector_band.shape[1]
    count = total // width
    half = latitude_taps.shape[0] // 2
    band_blocks = blocked_band(sector_band).astype(jnp.float32)

    def forward(member):
        coarse = member.astype(jnp.bfloat16)
        mixed = jnp.dot(vertical_root, coarse.reshape(levels, -1), preferred_element_type=jnp.float32)
        mixed = mixed.astype(jnp.bfloat16).reshape(levels, height, count, width)
        stacked = jnp.concatenate([jnp.roll(mixed, 1, axis=2), mixed, jnp.roll(mixed, -1, axis=2)], axis=3)
        spread = jnp.einsum('lybk,bkj->lybj', stacked.astype(jnp.float32), band_blocks)
        spread = lax.optimization_barrier(spread.astype(jnp.bfloat16)).reshape(levels, height, total)
        padded = jnp.pad(spread.astype(jnp.float32), ((0, 0), (half, half), (0, 0)))
        stencil = jnp.zeros((levels, height, total), jnp.float32)
        for offset in range(-half, half + 1):
            stencil = stencil + latitude_taps[offset + half][None, None, :] * padded[:, half + offset:half + offset + height, :]
        return stencil

    def accumulate(running, pair):
        member, perturb = pair
        return running + perturb.astype(jnp.float32) * forward(member), None

    increment, _ = lax.scan(accumulate, jnp.zeros((levels, height, total), jnp.float32), (control, ensemble))
    departure = inverse_error * (increment - innovation)

    def backward(pair):
        member, perturb = pair
        pulled = lax.optimization_barrier((perturb.astype(jnp.float32) * departure).astype(jnp.bfloat16))
        padded = jnp.pad(pulled.astype(jnp.float32), ((0, 0), (half, half), (0, 0)))
        spread_back = jnp.zeros((levels, height, total), jnp.float32)
        for offset in range(-half, half + 1):
            spread_back = spread_back + latitude_taps[offset + half][None, None, :] * padded[:, half - offset:half - offset + height, :]
        spread_back = spread_back.astype(jnp.bfloat16).reshape(levels, height, count, width)
        terms = jnp.einsum('lybj,bkj->lybk', spread_back.astype(jnp.float32), band_blocks)
        terms = lax.optimization_barrier(terms.astype(jnp.bfloat16)).astype(jnp.float32)
        summed = terms[..., width:2 * width] + jnp.roll(terms[..., 2 * width:], 1, axis=2) + jnp.roll(terms[..., :width], -1, axis=2)
        summed = summed.astype(jnp.bfloat16).reshape(levels, -1)
        returned = jnp.dot(vertical_root.T, summed, preferred_element_type=jnp.float32).astype(jnp.bfloat16)
        return member + returned.reshape(levels, height, total).astype(jnp.float32)

    gradient = lax.map(backward, (control, ensemble))
    return gradient, departure
```

```python
import functools

import jax
import jax.numpy as jnp
from jax import lax
from jax.experimental import pallas as pl
from jax.experimental.pallas import tpu as pltpu
from jax.sharding import PartitionSpec as P

F32, BF16 = jnp.float32, jnp.bfloat16
VMEM_LIMIT = 56 * 1024 * 1024


def lanes(block, width):
    return pl.ds(pl.multiple_of(block * width, width), width)


def vmem(count):
    return [pl.BlockSpec(memory_space=pltpu.VMEM)] * count


def vertical_block(fields, b, root, mixed, levels, height, width):
    pitch = mixed.shape[0] // height
    rows = jnp.concatenate(
        [fields[b, pl.ds(y, levels, stride=height), :] for y in range(height)], axis=1
    )
    out = jnp.dot(root[...], rows.astype(BF16), preferred_element_type=F32).astype(BF16)
    for y in range(height):
        mixed[y * pitch : y * pitch + levels, lanes(b, width)] = out[:, y * width : (y + 1) * width]


def longitude_block(b, blocks, bands, mixed, tile, levels, height, width):
    pitch = mixed.shape[0] // height
    parts = [mixed[:, lanes(lax.rem(b + blocks + o, blocks), width)] for o in (-1, 0, 1)]
    out = jnp.dot(jnp.concatenate(parts, axis=1), bands[b], preferred_element_type=F32)
    for y in range(height):
        tile[pl.ds(y, levels, stride=height), :] = out[y * pitch : y * pitch + levels]
    return tile[...].reshape(levels, height, width).astype(BF16)


def load_blocks(fields, k, held, sems, width, blocks):
    return [
        pltpu.make_async_copy(
            fields.at[k, :, pl.ds(b * width, width)], held.at[b], sems.at[b]
        )
        for b in range(blocks)
    ]


def forward_kernel(fields, root, bands, out, held, mixed, tile, sems, *, height, width):
    levels = root.shape[0]
    blocks = bands.shape[0]
    copies = load_blocks(fields, pl.program_id(0), held, sems, width, blocks)
    for copy in copies:
        copy.start()
    for b in range(blocks):
        copies[b].wait()
        vertical_block(held, b, root, mixed, levels, height, width)

    def longitude(b, _):
        out[b, 0] = longitude_block(b, blocks, bands, mixed, tile, levels, height, width)
        return 0

    lax.fori_loop(0, blocks, longitude, 0)


def row_index(width):
    return lax.broadcasted_iota(jnp.int32, (8, width), 0)


def forward_taps(taps, half, width):
    y = row_index(width)
    zero = jnp.zeros((8, width), F32)
    tap = lambda o: jnp.broadcast_to(taps[o + half : o + half + 1, :], (8, width))
    own, beyond = [tap(0)], [None]
    for r in range(1, 8):
        up = tap(r) if r <= half else zero
        down = tap(r - 8) if 8 - r <= half else zero
        own.append(jnp.where(y < 8 - r, up, down))
        beyond.append(jnp.where(y < 8 - r, down, up))
    return own, beyond


def stencil_level(spread, ensemble, beyond_ensemble, own_taps, beyond_taps):
    own = own_taps[0] * spread
    beyond = None
    for r in range(1, 8):
        turned = pltpu.roll(spread, 8 - r, 0)
        own = own + own_taps[r] * turned
        part = beyond_taps[r] * turned
        beyond = part if beyond is None else beyond + part
    return ensemble * own, beyond_ensemble * beyond


def stencil_kernel(spread, ensemble, edge, taps, up, down, own_sum, beyond_sum, *, half):
    members, levels, _, width = spread.shape
    own_taps, beyond_taps = forward_taps(taps, half, width)
    low = row_index(width) < 4

    def level(l, _):
        own = jnp.zeros((8, width), F32)
        beyond = jnp.zeros((8, width), F32)
        for k in range(members):
            a, b = stencil_level(
                spread[k, l].astype(F32),
                ensemble[k, l].astype(F32),
                edge[k, l].astype(F32),
                own_taps,
                beyond_taps,
            )
            own, beyond = own + a, beyond + b
        own_sum[l] = own
        beyond_sum[l] = beyond
        up[l] = jnp.where(low, beyond, own)
        down[l] = jnp.where(low, own, beyond)
        return 0

    lax.fori_loop(0, levels, level, 0)


def adjoint_level(own, beyond, taps, y):
    out = taps[0] * own
    for o, tap in taps.items():
        if o == 0:
            continue
        if o > 0:
            mixed = jnp.where(y < 8 - o, own, beyond)
        else:
            mixed = jnp.where(y >= -o, own, beyond)
        out = out + tap * pltpu.roll(mixed, o % 8, 0)
    return out


def adjoint_kernel(
    ensemble, edge, taps, own_sum, beyond_sum, below, above, innovation, inverse,
    edge_innovation, edge_inverse, departure, back, *, half
):
    members, levels, _, width = ensemble.shape
    y = row_index(width)
    low = y < 4
    tap = {
        o: jnp.broadcast_to(taps[o + half : o + half + 1, :], (8, width))
        for o in range(-half, half + 1)
    }

    def level(l, _):
        under, over = below[l], above[l]
        own = inverse[l] * (own_sum[l] + jnp.where(low, under, over) - innovation[l])
        beyond = edge_inverse[l] * (
            beyond_sum[l] + jnp.where(low, over, under) - edge_innovation[l]
        )
        departure[l] = own
        for k in range(members):
            a = (ensemble[k, l].astype(F32) * own).astype(BF16).astype(F32)
            b = (edge[k, l].astype(F32) * beyond).astype(BF16).astype(F32)
            back[k, l] = adjoint_level(a, b, tap, y).astype(BF16)
        return 0

    lax.fori_loop(0, levels, level, 0)


def adjoint_longitude(c, blocks, bands, flat, summed, width):
    before, after = lax.rem(c + blocks - 1, blocks), lax.rem(c + 1, blocks)
    left = jnp.concatenate([flat[:, lanes(b, width)] for b in (before, c, after)], axis=1)
    right = jnp.concatenate(
        [
            bands[before, 2 * width : 3 * width],
            bands[c, width : 2 * width],
            bands[after, 0:width],
        ],
        axis=1,
    )
    summed[c] = lax.dot_general(
        left, right, (((1,), (1,)), ((), ())), preferred_element_type=F32
    )


def adjoint_vertical(c, root, summed, held, levels, height, width):
    rows = [pl.ds(y, levels, stride=height) for y in range(height)]
    right = jnp.concatenate([summed[c, row, :] for row in rows], axis=1)
    out = lax.dot_general(
        root[...], right.astype(BF16), (((0,), (0,)), ((), ())), preferred_element_type=F32
    )
    out = out.astype(BF16).astype(F32)
    for y, row in enumerate(rows):
        held[c, row, :] = held[c, row, :] + out[:, y * width : (y + 1) * width]


def final_kernel(
    back, root, bands, control, gradient, held, flat, summed, in_sems, out_sems, *, height, width
):
    levels = root.shape[0]
    blocks = bands.shape[0]
    k = pl.program_id(0)
    copies = load_blocks(control, k, held, in_sems, width, blocks)
    for copy in copies:
        copy.start()

    def place(b, _):
        rows = back[b, 0].astype(F32).reshape(levels * height, width)
        flat[:, lanes(b, width)] = rows.astype(BF16)
        return 0

    lax.fori_loop(0, blocks, place, 0)

    def longitude(c, _):
        adjoint_longitude(c, blocks, bands, flat, summed, width)
        return 0

    lax.fori_loop(0, blocks, longitude, 0)
    stores = [
        pltpu.make_async_copy(
            held.at[b], gradient.at[k, :, pl.ds(b * width, width)], out_sems.at[b]
        )
        for b in range(blocks)
    ]
    for c in range(blocks):
        copies[c].wait()
        adjoint_vertical(c, root, summed, held, levels, height, width)
        stores[c].start()
    for store in stores:
        store.wait()


def shards(control, ensemble, vertical_root, sector_band, latitude_taps, innovation, inverse_error):
    half = latitude_taps.shape[0] // 2
    width = sector_band.shape[1]
    own, levels, height, total = control.shape
    members = ensemble.shape[0]
    blocks = total // width
    lats = lax.axis_size("lat")
    forward = [(i, i + 1) for i in range(lats - 1)]
    backward = [(i + 1, i) for i in range(lats - 1)]
    params = pltpu.CompilerParams(vmem_limit_bytes=VMEM_LIMIT)

    bands = lax.all_gather(sector_band, "lon", axis=0, tiled=False)
    bands = bands.reshape(blocks, 3 * width, width)

    def edges(array, dim):
        mid = height // 2
        low = lax.ppermute(lax.slice_in_dim(array, 0, mid, axis=dim), "lat", backward)
        high = lax.ppermute(lax.slice_in_dim(array, mid, height, axis=dim), "lat", forward)
        return jnp.concatenate([low, high], axis=dim)

    edge = edges(ensemble, 2)
    edge_innovation, edge_inverse = edges(innovation, 1), edges(inverse_error, 1)

    fields = control.reshape(own, levels * height, total)
    pitch = -(-levels // 16) * 16
    whole = lambda *shape: pl.BlockSpec(shape, lambda k: (0,) * len(shape))
    spread = pl.pallas_call(
        functools.partial(forward_kernel, height=height, width=width),
        grid=(own,),
        in_specs=[
            pl.BlockSpec(memory_space=pl.ANY),
            whole(levels, levels),
            whole(blocks, 3 * width, width),
        ],
        out_specs=pl.BlockSpec((blocks, 1, levels, height, width), lambda k: (0, k, 0, 0, 0)),
        out_shape=jax.ShapeDtypeStruct((blocks, own, levels, height, width), BF16),
        scratch_shapes=[
            pltpu.VMEM((blocks, levels * height, width), F32),
            pltpu.VMEM((height * pitch, total), BF16),
            pltpu.VMEM((levels * height, width), F32),
            pltpu.SemaphoreType.DMA((blocks,)),
        ],
        compiler_params=params,
        name="spread",
    )(fields, vertical_root, bands)
    spread = lax.all_to_all(spread, "lon", split_axis=0, concat_axis=0, tiled=True)
    spread = spread.reshape(members, levels, height, width)
    sums = jax.ShapeDtypeStruct((levels, height, width), F32)
    up, down, own_sum, beyond_sum = pl.pallas_call(
        functools.partial(stencil_kernel, half=half),
        in_specs=vmem(4),
        out_specs=vmem(4),
        out_shape=[sums] * 4,
        compiler_params=params,
        name="stencil",
    )(spread, ensemble, edge, latitude_taps)
    below = lax.ppermute(up, "lat", forward)
    above = lax.ppermute(down, "lat", backward)
    departure, back = pl.pallas_call(
        functools.partial(adjoint_kernel, half=half),
        in_specs=vmem(11),
        out_specs=vmem(2),
        out_shape=[sums, jax.ShapeDtypeStruct((members, levels, height, width), BF16)],
        compiler_params=params,
        name="adjoint",
    )(
        ensemble, edge, latitude_taps, own_sum, beyond_sum, below, above, innovation,
        inverse_error, edge_innovation, edge_inverse,
    )
    back = back.reshape(blocks, own, levels, height, width)
    back = lax.all_to_all(back, "lon", split_axis=0, concat_axis=0, tiled=True)
    gradient = pl.pallas_call(
        functools.partial(final_kernel, height=height, width=width),
        grid=(own,),
        in_specs=[
            pl.BlockSpec((blocks, 1, levels, height, width), lambda k: (0, k, 0, 0, 0)),
            whole(levels, levels),
            whole(blocks, 3 * width, width),
            pl.BlockSpec(memory_space=pl.ANY),
        ],
        out_specs=pl.BlockSpec(memory_space=pl.ANY),
        out_shape=jax.ShapeDtypeStruct((own, levels * height, total), F32),
        scratch_shapes=[
            pltpu.VMEM((blocks, levels * height, width), F32),
            pltpu.VMEM((levels * height, total), BF16),
            pltpu.VMEM((blocks, levels * height, width), F32),
            pltpu.SemaphoreType.DMA((blocks,)),
            pltpu.SemaphoreType.DMA((blocks,)),
        ],
        compiler_params=params,
        name="final",
    )(back, vertical_root, bands, fields)
    return gradient.reshape(control.shape), departure


def solution(mesh):
    placed = (
        P("lon", None, "lat", None),
        P(None, None, "lat", "lon"),
        P(),
        P(None, None, "lon"),
        P(None, "lon"),
        P(None, "lat", "lon"),
        P(None, "lat", "lon"),
    )
    return jax.shard_map(
        shards,
        mesh=mesh,
        in_specs=placed,
        out_specs=(P("lon", None, "lat", None), P(None, "lat", "lon")),
        check_vma=False,
    )
```

```python
import functools

import jax
import jax.numpy as jnp
from jax import lax
from jax.experimental import pallas as pl
from jax.experimental.pallas import tpu as pltpu
from jax.sharding import PartitionSpec as P

F32, BF16 = jnp.float32, jnp.bfloat16
VMEM_LIMIT = 62 * 1024 * 1024


def lanes(block, width):
    return pl.ds(pl.multiple_of(block * width, width), width)


def vertical_block(fields, b, root, mixed, levels, height, width):
    pitch = mixed.shape[0] // height
    rows = jnp.concatenate(
        [fields[b, pl.ds(y, levels, stride=height), :] for y in range(height)], axis=1
    )
    out = jnp.dot(root[...], rows.astype(BF16), preferred_element_type=F32).astype(BF16)
    for y in range(height):
        mixed[y * pitch : y * pitch + levels, lanes(b, width)] = out[:, y * width : (y + 1) * width]


def longitude_block(b, blocks, bands, mixed, tile, levels, height, width):
    pitch = mixed.shape[0] // height
    parts = [mixed[:, lanes(lax.rem(b + blocks + o, blocks), width)] for o in (-1, 0, 1)]
    out = jnp.dot(jnp.concatenate(parts, axis=1), bands[b], preferred_element_type=F32)
    for y in range(height):
        tile[pl.ds(y, levels, stride=height), :] = out[y * pitch : y * pitch + levels]
    return tile[...].reshape(levels, height, width).astype(BF16)


def row_index(width):
    return lax.broadcasted_iota(jnp.int32, (8, width), 0)


def forward_taps(taps, half, width):
    y = row_index(width)
    zero = jnp.zeros((8, width), F32)
    tap = lambda o: jnp.broadcast_to(taps[o + half : o + half + 1, :], (8, width))
    own, beyond = [tap(0)], [None]
    for r in range(1, 8):
        up = tap(r) if r <= half else zero
        down = tap(r - 8) if 8 - r <= half else zero
        own.append(jnp.where(y < 8 - r, up, down))
        beyond.append(jnp.where(y < 8 - r, down, up))
    return own, beyond


def stencil_level(spread, ensemble, beyond_ensemble, own_taps, beyond_taps):
    own = own_taps[0] * spread
    beyond = None
    for r in range(1, 8):
        turned = pltpu.roll(spread, 8 - r, 0)
        own = own + own_taps[r] * turned
        part = beyond_taps[r] * turned
        beyond = part if beyond is None else beyond + part
    return ensemble * own, beyond_ensemble * beyond


def adjoint_level(own, beyond, taps, y):
    out = taps[0] * own
    for o, tap in taps.items():
        if o == 0:
            continue
        if o > 0:
            mixed = jnp.where(y < 8 - o, own, beyond)
        else:
            mixed = jnp.where(y >= -o, own, beyond)
        out = out + tap * pltpu.roll(mixed, o % 8, 0)
    return out


def adjoint_longitude(c, blocks, bands, flat, summed, width):
    before, after = lax.rem(c + blocks - 1, blocks), lax.rem(c + 1, blocks)
    left = jnp.concatenate([flat[:, lanes(b, width)] for b in (before, c, after)], axis=1)
    right = jnp.concatenate(
        [
            bands[before, 2 * width : 3 * width],
            bands[c, width : 2 * width],
            bands[after, 0:width],
        ],
        axis=1,
    )
    summed[c] = lax.dot_general(
        left, right, (((1,), (1,)), ((), ())), preferred_element_type=F32
    )


def adjoint_vertical(c, root, summed, held, levels, height, width):
    rows = [pl.ds(y, levels, stride=height) for y in range(height)]
    right = jnp.concatenate([summed[c, row, :] for row in rows], axis=1)
    out = lax.dot_general(
        root[...], right.astype(BF16), (((0,), (0,)), ((), ())), preferred_element_type=F32
    )
    out = out.astype(BF16).astype(F32)
    for y, row in enumerate(rows):
        held[c, row, :] = held[c, row, :] + out[:, y * width : (y + 1) * width]


def program(
    fields, ensemble, root, band, taps, innovation, inverse, gradient, departure,
    held, mixed, tile, bands, send, spread, back, flat, summed,
    up, down, below, above, fact_up, fact_down, fact_below, fact_above,
    sum_up, sum_down, sum_below, sum_above, own_sum, beyond_sum,
    load_sem, store_sem, band_sems, spread_sems, back_sems, up_sems, down_sems,
    fact_sems, sum_sems, *, half
):
    members, levels, height, width = ensemble.shape
    own = fields.shape[0]
    blocks = bands.shape[0]
    me, row = lax.axis_index("lon"), lax.axis_index("lat")
    has_below, has_above = row > 0, row < lax.axis_size("lat") - 1
    mid = levels // 2
    y = row_index(width)
    low = y < 4

    def remote(source, target, sems, index, **device):
        return pltpu.make_async_remote_copy(
            src_ref=source, dst_ref=target,
            send_sem=sems.at[(0,) + index], recv_sem=sems.at[(1,) + index],
            device_id=device, device_id_type=pl.DeviceIdType.MESH,
        )

    def loop(start, stop, body, unroll=1):
        def step(i, _):
            body(i)
            return 0

        lax.fori_loop(start, stop, step, 0, unroll=unroll)

    def load(k, b):
        return pltpu.make_async_copy(
            fields.at[k, :, lanes(b, width)], held.at[k, b], load_sem.at[k, b]
        )

    def store(k, b):
        return pltpu.make_async_copy(
            held.at[k, b], gradient.at[k, :, lanes(b, width)], store_sem.at[k, b]
        )

    def to_above(source, target, sems, index):
        return remote(source, target, sems, index, lat=row + 1)

    def to_below(source, target, sems, index):
        return remote(source, target, sems, index, lat=row - 1)

    def both(action, pairs):
        for guard, copy in pairs:
            @pl.when(guard)
            def _():
                action(copy())

    for k in range(own):
        loop(0, blocks, lambda b: load(k, b).start())
    barrier = pltpu.get_barrier_semaphore()
    loop(1, blocks, lambda t: pl.semaphore_signal(
        barrier, inc=1, device_id={"lon": lax.rem(me + t, blocks)},
        device_id_type=pl.DeviceIdType.MESH))

    @pl.when(has_below)
    def _():
        pl.semaphore_signal(barrier, inc=1, device_id={"lat": row - 1},
                            device_id_type=pl.DeviceIdType.MESH)

    @pl.when(has_above)
    def _():
        pl.semaphore_signal(barrier, inc=1, device_id={"lat": row + 1},
                            device_id_type=pl.DeviceIdType.MESH)

    inner = jnp.logical_and(has_below, has_above)

    @pl.when(inner)
    def _():
        pl.semaphore_wait(barrier, blocks + 1)

    @pl.when(jnp.logical_not(inner))
    def _():
        pl.semaphore_wait(barrier, blocks)

    def band_send(t):
        target = lax.rem(me + t, blocks)
        pltpu.make_async_remote_copy(
            src_ref=band, dst_ref=bands.at[me], send_sem=band_sems.at[0, target],
            recv_sem=band_sems.at[1, me], device_id={"lon": target},
            device_id_type=pl.DeviceIdType.MESH,
        ).start()

    def band_wait(source):
        return pltpu.make_async_remote_copy(
            src_ref=band, dst_ref=bands.at[source], send_sem=band_sems.at[0, source],
            recv_sem=band_sems.at[1, source], device_id={"lon": source},
            device_id_type=pl.DeviceIdType.MESH,
        )

    loop(1, blocks, band_send)
    bands[me] = band[...]

    tiles = levels - mid

    def fold(a, b):
        return jnp.where(low, pltpu.roll(b, 4, 0), a), jnp.where(low, a, pltpu.roll(b, 4, 0))

    def unfold(under, over):
        return (
            jnp.where(low, over, under),
            pltpu.roll(jnp.where(low, under, over), 4, 0),
        )

    def edge_copies(k):
        return (
            (has_above, lambda: to_above(up.at[k], below.at[k], up_sems, (k,))),
            (has_below, lambda: to_below(down.at[k], above.at[k], down_sems, (k,))),
        )

    def edge_arrivals(k):
        return (
            (has_below, lambda: to_below(up.at[k], below.at[k], up_sems, (k,))),
            (has_above, lambda: to_above(down.at[k], above.at[k], down_sems, (k,))),
        )

    def edge_member(t, k):
        member = lax.rem(me + blocks - t, blocks) * own + k

        def pack(l):
            a, b = ensemble[member, l].astype(F32), ensemble[member, l + mid].astype(F32)
            high, bottom = fold(a, b)
            up[member, l] = high.astype(BF16)
            down[member, l] = bottom.astype(BF16)

        loop(0, tiles, pack)
        both(lambda copy: copy.start(), edge_copies(member))

    for k in range(own):
        loop(0, blocks, lambda t: edge_member(t, k))

    fact_copies = (
        (has_above, lambda: to_above(fact_up, fact_below, fact_sems, (0,))),
        (has_below, lambda: to_below(fact_down, fact_above, fact_sems, (1,))),
    )
    fact_arrivals = (
        (has_below, lambda: to_below(fact_up, fact_below, fact_sems, (0,))),
        (has_above, lambda: to_above(fact_down, fact_above, fact_sems, (1,))),
    )

    def pack_facts(l):
        fact_up[l], fact_down[l] = fold(innovation[l], inverse[l])

    loop(0, levels, pack_facts)
    both(lambda copy: copy.start(), fact_copies)

    @pl.when(row == 0)
    def _():
        def clear(k):
            below[k] = jnp.zeros(below.shape[1:], BF16)

        loop(0, members, clear)
        fact_below[...] = jnp.zeros(fact_below.shape, F32)
        sum_below[...] = jnp.zeros(sum_below.shape, F32)

    @pl.when(row == lax.axis_size("lat") - 1)
    def _():
        def clear(k):
            above[k] = jnp.zeros(above.shape[1:], BF16)

        loop(0, members, clear)
        fact_above[...] = jnp.zeros(fact_above.shape, F32)
        sum_above[...] = jnp.zeros(sum_above.shape, F32)

    def exchange(source, target, sems, k, peer):
        return pltpu.make_async_remote_copy(
            src_ref=source.at[peer, k], dst_ref=target.at[me, k],
            send_sem=sems.at[0, k, peer], recv_sem=sems.at[1, k, me],
            device_id={"lon": peer}, device_id_type=pl.DeviceIdType.MESH,
        )

    def arrival(source, target, sems, k, peer):
        return pltpu.make_async_remote_copy(
            src_ref=source.at[peer, k], dst_ref=target.at[peer, k],
            send_sem=sems.at[0, k, peer], recv_sem=sems.at[1, k, peer],
            device_id={"lon": peer}, device_id_type=pl.DeviceIdType.MESH,
        )

    for k in range(own):
        def vertical(b):
            load(k, b).wait()
            vertical_block(held.at[k], b, root, mixed, levels, height, width)

        loop(0, blocks, vertical)
        if k == 0:
            loop(1, blocks, lambda t: band_wait(lax.rem(me + t, blocks)).wait_recv())

        def longitude(t):
            b = lax.rem(me + t, blocks)
            value = longitude_block(b, blocks, bands, mixed, tile, levels, height, width)

            @pl.when(t < blocks)
            def _():
                send[b, k] = value
                exchange(send, spread, spread_sems, k, b).start()

            @pl.when(t == blocks)
            def _():
                spread[b, k] = value

        loop(1, blocks + 1, longitude)

    own_taps, beyond_taps = forward_taps(taps, half, width)

    def clear_sums(l):
        own_sum[l] = jnp.zeros((8, width), F32)
        beyond_sum[l] = jnp.zeros((8, width), F32)

    loop(0, levels, clear_sums)

    def stencil(t, k):
        source = lax.rem(me + blocks - t, blocks)
        member = source * own + k

        @pl.when(t > 0)
        def _():
            arrival(send, spread, spread_sems, k, source).wait_recv()

        both(lambda copy: copy.wait_recv(), edge_arrivals(member))

        def add(l, beyond_ensemble):
            a, b = stencil_level(
                spread[source, k, l].astype(F32), ensemble[member, l].astype(F32),
                beyond_ensemble, own_taps, beyond_taps,
            )
            own_sum[l] += a
            beyond_sum[l] += b

        def two(l):
            first, second = unfold(below[member, l].astype(F32), above[member, l].astype(F32))
            add(l, first)
            add(l + mid, second)

        loop(0, mid, two, 2 if mid % 2 == 0 else 1)
        if levels % 2:
            _, second = unfold(below[member, mid].astype(F32), above[member, mid].astype(F32))
            add(levels - 1, second)

    for k in range(own):
        loop(0, blocks, lambda t: stencil(t, k))

    def boundary(l):
        own_part, beyond_part = own_sum[l], beyond_sum[l]
        sum_up[l] = jnp.where(low, beyond_part, own_part)
        sum_down[l] = jnp.where(low, own_part, beyond_part)

    loop(0, levels, boundary)
    sum_copies = (
        (has_above, lambda: to_above(sum_up, sum_below, sum_sems, (0,))),
        (has_below, lambda: to_below(sum_down, sum_above, sum_sems, (1,))),
    )
    sum_arrivals = (
        (has_below, lambda: to_below(sum_up, sum_below, sum_sems, (0,))),
        (has_above, lambda: to_above(sum_down, sum_above, sum_sems, (1,))),
    )
    both(lambda copy: copy.start(), sum_copies)
    both(lambda copy: copy.wait_recv(), fact_arrivals)
    both(lambda copy: copy.wait_recv(), sum_arrivals)

    def depart(l):
        under, over = sum_below[l], sum_above[l]
        edge_innovation, edge_inverse = unfold(fact_below[l], fact_above[l])
        value = inverse[l] * (own_sum[l] + jnp.where(low, under, over) - innovation[l])
        departure[l] = value
        own_sum[l] = value
        beyond_sum[l] = edge_inverse * (
            beyond_sum[l] + jnp.where(low, over, under) - edge_innovation
        )

    loop(0, levels, depart)

    tap = {
        o: jnp.broadcast_to(taps[o + half : o + half + 1, :], (8, width))
        for o in range(-half, half + 1)
    }

    def adjoint(t, k):
        target = lax.rem(me + t, blocks)
        member = target * own + k

        def write(l, beyond_ensemble):
            a = (ensemble[member, l].astype(F32) * own_sum[l]).astype(BF16).astype(F32)
            b = (beyond_ensemble * beyond_sum[l]).astype(BF16).astype(F32)
            spread[target, k, l] = adjoint_level(a, b, tap, y).astype(BF16)

        def two(l):
            first, second = unfold(below[member, l].astype(F32), above[member, l].astype(F32))
            write(l, first)
            write(l + mid, second)

        loop(0, mid, two, 2 if mid % 2 == 0 else 1)
        if levels % 2:
            _, second = unfold(below[member, mid].astype(F32), above[member, mid].astype(F32))
            write(levels - 1, second)

        @pl.when(t < blocks)
        def _():
            exchange(spread, back, back_sems, k, target).start()

    for k in range(own):
        loop(1, blocks + 1, lambda t: adjoint(t, k))

    for k in range(own):
        def place(t):
            source = lax.rem(me + blocks - t, blocks)

            def put(value):
                rows = value.astype(F32).reshape(levels * height, width)
                flat[:, lanes(source, width)] = rows.astype(BF16)

            @pl.when(t == 0)
            def _():
                put(spread[source, k])

            @pl.when(t > 0)
            def _():
                arrival(spread, back, back_sems, k, source).wait_recv()
                put(back[source, k])

        loop(0, blocks, place)
        loop(0, blocks, lambda c: adjoint_longitude(c, blocks, bands, flat, summed, width))

        def finish(c):
            adjoint_vertical(c, root, summed, held.at[k], levels, height, width)
            store(k, c).start()

        loop(0, blocks, finish)

    for k in range(own):
        loop(0, blocks, lambda b: store(k, b).wait())

        def sent(t):
            peer = lax.rem(me + t, blocks)
            exchange(send, spread, spread_sems, k, peer).wait_send()
            exchange(spread, back, back_sems, k, peer).wait_send()

        loop(1, blocks, sent)
    loop(1, blocks, lambda t: band_wait(lax.rem(me + t, blocks)).wait_send())
    loop(0, members, lambda k: both(lambda copy: copy.wait_send(), edge_copies(k)))
    both(lambda copy: copy.wait_send(), fact_copies)
    both(lambda copy: copy.wait_send(), sum_copies)


def shards(control, ensemble, vertical_root, sector_band, latitude_taps, innovation, inverse_error):
    half = latitude_taps.shape[0] // 2
    width = sector_band.shape[1]
    own, levels, height, total = control.shape
    members = ensemble.shape[0]
    blocks = total // width
    pitch = -(-levels // 16) * 16
    tiles = levels - levels // 2
    rows = levels * height
    fields = control.reshape(own, rows, total)
    band = sector_band.reshape(3 * width, width)
    sums = (levels, height, width)
    dma = pltpu.SemaphoreType.DMA
    local = pl.BlockSpec(memory_space=pltpu.VMEM)
    remote = pl.BlockSpec(memory_space=pl.ANY)
    gradient, departure = pl.pallas_call(
        functools.partial(program, half=half),
        in_specs=[remote] + [local] * 6,
        out_specs=[remote, local],
        out_shape=[
            jax.ShapeDtypeStruct((own, rows, total), F32),
            jax.ShapeDtypeStruct(sums, F32),
        ],
        scratch_shapes=[
            pltpu.VMEM((own, blocks, rows, width), F32),
            pltpu.VMEM((height * pitch, total), BF16),
            pltpu.VMEM((rows, width), F32),
            pltpu.VMEM((blocks, 3 * width, width), BF16),
            pltpu.VMEM((blocks, own) + sums, BF16),
            pltpu.VMEM((blocks, own) + sums, BF16),
            pltpu.VMEM((blocks, own) + sums, BF16),
            pltpu.VMEM((rows, total), BF16),
            pltpu.VMEM((blocks, rows, width), F32),
        ]
        + [pltpu.VMEM((members, tiles, height, width), BF16)] * 4
        + [pltpu.VMEM(sums, F32)] * 10
        + [
            dma((own, blocks)),
            dma((own, blocks)),
            dma((2, blocks)),
            dma((2, own, blocks)),
            dma((2, own, blocks)),
            dma((2, members)),
            dma((2, members)),
            dma((2, 2)),
            dma((2, 2)),
        ],
        compiler_params=pltpu.CompilerParams(
            vmem_limit_bytes=VMEM_LIMIT, collective_id=0, has_side_effects=True
        ),
        name="gradient",
    )(fields, ensemble, vertical_root, band, latitude_taps, innovation, inverse_error)
    return gradient.reshape(control.shape), departure


def solution(mesh):
    placed = (
        P("lon", None, "lat", None),
        P(None, None, "lat", "lon"),
        P(),
        P(None, None, "lon"),
        P(None, "lon"),
        P(None, "lat", "lon"),
        P(None, "lat", "lon"),
    )
    return jax.shard_map(
        shards,
        mesh=mesh,
        in_specs=placed,
        out_specs=(P("lon", None, "lat", None), P(None, "lat", "lon")),
        check_vma=False,
    )
```
